32 devices in a mesh: seq: 8 (over z, y), head: 4 (over x, core).
Axes of the slice: x: 2, y: 2, z: 4, core: 2. Of those that a mesh axis runs over, the one named last changes fastest.
Arguments:
- x_in: bfloat16 [4096, 1024], P('seq', 'head'), may hold values from -6 to 6
- in_gain: float32 [1024], replicated, may hold values from 0.5 to 1.5
- w_zx: bfloat16 [1024, 2, 2048], P(None, None, 'head'), may hold values from -0.1875 to 0.1875
- w_dt: bfloat16 [1024, 32], P(None, 'head'), may hold values from -0.1875 to 0.1875
- w_bc: bfloat16 [1024, 256], replicated, may hold values from -0.1875 to 0.1875
- conv_x: float32 [4, 2048], P(None, 'head'), may hold values from -3 to 3
- conv_x_bias: float32 [2048], P('head'), may hold values from -0.5 to 0.5
- conv_bc: float32 [4, 256], replicated, may hold values from -3 to 3
- conv_bc_bias: float32 [256], replicated, may hold values from -0.5 to 0.5
- a_log: float32 [32], P('head'), may hold values from -7 to 0.7
- dt_bias: float32 [32], P('head'), may hold values from -6 to -2
- d_skip: float32 [32], P('head'), may hold values from 0.5 to 1.5
- norm_scale: float32 [2048], P('head'), may hold values from 0.5 to 1.5
- w_out: bfloat16 [2048, 1024], P('head'), may hold values from -0.125 to 0.125
- cotangent: bfloat16 [4096, 1024], P('seq', 'head'), may hold values from -6 to 6
Outputs:
- y_out: bfloat16 [4096, 1024], P('seq', 'head')
- d_x_in: float32 [4096, 1024], P('seq', 'head')
- g_in_gain: float32 [1024], P('head')
- g_w_zx: float32 [1024, 2, 2048], P(None, None, 'head')
- g_w_dt: float32 [1024, 32], P(None, 'head')
- g_w_bc: float32 [1024, 256], replicated
- g_conv_x: float32 [4, 2048], P(None, 'head')
- g_conv_x_bias: float32 [2048], P('head')
- g_conv_bc: float32 [4, 256], replicated
- g_conv_bc_bias: float32 [256], replicated
- g_a_log: float32 [32], P('head')
- g_dt_bias: float32 [32], P('head')
- g_d_skip: float32 [32], P('head')
- g_norm_scale: float32 [2048], P('head')
- g_w_out: float32 [2048, 1024], P('head')
The draws below stay inside these ranges and needn't reach their ends.
All inputs are finite; a program needn't handle non-finite values.
Results may differ from the reference program's by a relative error of at most 0.002.
The reference program's roundings to bfloat16 on the way (of `normed`, `proj_zx`, `bc_raw`, `activated`, `gate_normed` and `d_zx`) count: a program that leaves them out, or rounds other values in their place, can miss the bound.
Values may be sent and summed in bfloat16 or wider, within the bound.
No kernel may reach another device: no remote copies, remote signals or barrier semaphores. Data moves between devices by JAX's collectives and lax.ppermute only.
A program may use at most 128 MiB of HBM per device.

```python
import jax
import jax.numpy as jnp
from jax import lax

D = 1024
HEADS = 32
HEADDIM = 64
STATE = 128
CONV = 4
GROUP = 256
INNER = 2048
SEQLEN = 4096


def levels(stream_key, shape, shards, least, high):
    def one(position, parts):
        steps = jax.random.uniform(jax.random.fold_in(jax.random.fold_in(stream_key, 6), position), (parts,), jnp.float32, least / len(shards), high / len(shards))
        return jnp.repeat(jnp.exp(steps), shape[position] // parts).reshape((-1,) + (1,) * (len(shape) - position - 1))

    gain = one(*shards[0])
    for cut in shards[1:]:
        gain = gain * one(*cut)
    return gain


def centred(rng, extent, scale, reach, cuts=(), held_as=jnp.bfloat16):
    factor_of = levels(rng, extent, cuts, -0.22, 0.18) if cuts else 1.0
    drawn = jax.random.normal(rng, extent, jnp.float32) * scale * factor_of
    return jnp.minimum(jnp.maximum(drawn, -reach), reach).astype(held_as)


def setup_inputs(seed: int = 0) -> dict:
    keys = jax.random.split(jax.random.key(seed), 16)
    x_in = centred(keys[0], (SEQLEN, D), 1.0, 6.0, ((0, 8), (1, 4)))
    in_gain = jnp.clip(1.0 + 0.1 * jax.random.normal(keys[1], (D,), jnp.float32), 0.5, 1.5)
    w_zx = centred(keys[2], (D, 2, INNER), D ** -0.5, 0.1875, ((2, 4),))
    w_dt = centred(keys[3], (D, HEADS), D ** -0.5, 0.1875, ((1, 4),))
    w_bc = centred(keys[4], (D, 2 * STATE), D ** -0.5, 0.1875)
    conv_x = centred(keys[5], (CONV, INNER), CONV ** -0.5, 3.0, ((1, 4),), jnp.float32)
    conv_x_bias = jnp.clip(jax.random.uniform(keys[6], (INNER,), jnp.float32, -0.5, 0.5) * levels(keys[6], (INNER,), ((0, 4),), -0.4, 0.0), -0.5, 0.5)
    conv_bc = centred(keys[7], (CONV, 2 * STATE), CONV ** -0.5, 3.0, (), jnp.float32)
    conv_bc_bias = jnp.clip(jax.random.uniform(keys[8], (2 * STATE,), jnp.float32, -0.5, 0.5), -0.5, 0.5)
    a_log = jnp.clip(-7.0 + 7.7 * jax.random.uniform(keys[9], (HEADS,), jnp.float32) ** levels(keys[9], (HEADS,), ((0, 4),), -0.2, 0.2), -7.0, 0.7)
    dt_bias = jnp.clip(-6.0 + 4.0 * jax.random.uniform(keys[10], (HEADS,), jnp.float32) ** levels(keys[10], (HEADS,), ((0, 4),), -0.2, 0.2), -6.0, -2.0)
    d_skip = jnp.clip(0.5 + 1.0 * jax.random.uniform(keys[11], (HEADS,), jnp.float32) ** levels(keys[11], (HEADS,), ((0, 4),), -0.2, 0.2), 0.5, 1.5)
    norm_scale = jnp.clip(1.0 + 0.1 * jax.random.normal(keys[12], (INNER,), jnp.float32), 0.5, 1.5)
    w_out = centred(keys[13], (INNER, D), INNER ** -0.5, 0.125, ((0, 4),))
    cotangent = centred(keys[14], (SEQLEN, D), 1.0, 6.0, ((0, 8), (1, 4)))
    return {"x_in": x_in, "in_gain": in_gain, "w_zx": w_zx, "w_dt": w_dt, "w_bc": w_bc, "conv_x": conv_x, "conv_x_bias": conv_x_bias, "conv_bc": conv_bc, "conv_bc_bias": conv_bc_bias, "a_log": a_log, "dt_bias": dt_bias, "d_skip": d_skip, "norm_scale": norm_scale, "w_out": w_out, "cotangent": cotangent}


EPSILON = 1e-05
PRECISE = lax.Precision.HIGHEST

def ssd_span(x_vals, b_vals, c_vals, step_size, decay_rates, skip_gain, start_state):
    row_count, head_count, head_width = x_vals.shape
    block_count = row_count // GROUP
    lower_mask = jnp.arange(GROUP)[:, None] >= jnp.arange(GROUP)[None, :]

    def one_block(carried, block_in):
        x_block, b_block, c_block, step_block = block_in
        cumulative = jnp.cumsum(step_block * decay_rates[None, :], axis=0)
        scores = jnp.dot(c_block, b_block.T, precision=PRECISE)
        spread = cumulative.T[:, :, None] - cumulative.T[:, None, :]
        decays = jnp.exp(jnp.where(lower_mask[None], spread, -1e+30))
        mixing = scores[None] * decays * step_block.T[:, None, :]
        within = jnp.einsum('hts,shp->thp', mixing, x_block, precision=PRECISE)
        earlier = jnp.exp(cumulative)[:, :, None] * jnp.einsum('tn,hpn->thp', c_block, carried, precision=PRECISE)
        toward = jnp.exp(cumulative[-1:] - cumulative) * step_block
        fresh_state = jnp.einsum('thp,tn->hpn', x_block * toward[:, :, None], b_block, precision=PRECISE)
        carried = jnp.exp(cumulative[-1])[:, None, None] * carried + fresh_state
        return (carried, within + earlier + skip_gain[None, :, None] * x_block)
    block_inputs = (x_vals.reshape(block_count, GROUP, head_count, head_width), b_vals.reshape(block_count, GROUP, b_vals.shape[1]), c_vals.reshape(block_count, GROUP, c_vals.shape[1]), step_size.reshape(block_count, GROUP, head_count))
    final_state, outputs = lax.scan(jax.checkpoint(one_block), start_state, block_inputs)
    return (outputs.reshape(row_count, head_count, head_width), final_state)

def conv_act(padded, weights, biases):
    row_count = padded.shape[0] - weights.shape[0] + 1
    summed = jnp.zeros((row_count, padded.shape[1]), jnp.float32) + biases[None, :]
    for offset in range(weights.shape[0]):
        summed = summed + weights[offset][None, :] * padded[offset:offset + row_count]
    return jax.nn.silu(summed)

def reference(x_in, in_gain, w_zx, w_dt, w_bc, conv_x, conv_x_bias, conv_bc, conv_bc_bias, a_log, dt_bias, d_skip, norm_scale, w_out, cotangent):
    row_count = x_in.shape[0]
    inner_total = w_zx.shape[2]
    head_count = w_dt.shape[1]
    input_float = x_in.astype(jnp.float32)
    inv_rms = lax.rsqrt(lax.optimization_barrier(jnp.mean(input_float * input_float, axis=1, keepdims=True)) + EPSILON)
    normed = (input_float * inv_rms * in_gain[None, :]).astype(jnp.bfloat16)
    flat_weight = w_zx.reshape(w_zx.shape[0], 2 * inner_total)
    proj_zx = jnp.dot(normed, flat_weight, preferred_element_type=jnp.float32).astype(jnp.bfloat16)
    dt_raw = jnp.dot(normed, w_dt, preferred_element_type=jnp.float32)
    bc_raw = jnp.dot(normed, w_bc, preferred_element_type=jnp.float32).astype(jnp.bfloat16)
    gate_in = proj_zx[:, :inner_total].astype(jnp.float32)
    pre_conv = jnp.concatenate([proj_zx[:, inner_total:], bc_raw], axis=1)
    conv_w = jnp.concatenate([conv_x, conv_bc], axis=1)
    conv_b = jnp.concatenate([conv_x_bias, conv_bc_bias])
    padded = jnp.concatenate([jnp.zeros((CONV - 1, pre_conv.shape[1]), jnp.float32), pre_conv.astype(jnp.float32)], axis=0)
    activated = conv_act(padded, conv_w, conv_b).astype(jnp.bfloat16)
    act_float = activated.astype(jnp.float32)
    x_heads = act_float[:, :inner_total].reshape(row_count, head_count, HEADDIM)
    b_vals = act_float[:, inner_total:inner_total + STATE]
    c_vals = act_float[:, inner_total + STATE:]
    step_size = jax.nn.softplus(dt_raw + dt_bias[None, :])
    decay_rates = -jnp.exp(a_log)
    zero_state = jnp.zeros((head_count, HEADDIM, STATE), jnp.float32)

    def ssd_only(x_part, b_part, c_part, step_part, rate_part, skip_part):
        return ssd_span(x_part, b_part, c_part, step_part, rate_part, skip_part, zero_state)[0]
    ssd_out, pull_ssd = jax.vjp(ssd_only, x_heads, b_vals, c_vals, step_size, decay_rates, d_skip)
    ssd_flat = ssd_out.reshape(row_count, inner_total)
    sig_z = jax.nn.sigmoid(gate_in)
    gated_rows = ssd_flat * gate_in * sig_z
    inv_gate = lax.rsqrt(lax.optimization_barrier(jnp.mean(gated_rows * gated_rows, axis=1, keepdims=True)) + EPSILON)
    gate_normed = (gated_rows * inv_gate * norm_scale[None, :]).astype(jnp.bfloat16)
    y_out = (input_float + jnp.dot(gate_normed, w_out, preferred_element_type=jnp.float32)).astype(jnp.bfloat16)
    d_gn = jnp.dot(cotangent, w_out.T, preferred_element_type=jnp.float32)
    g_w_out = jnp.dot(gate_normed.T, cotangent, preferred_element_type=jnp.float32)
    g_norm_scale = lax.optimization_barrier(jnp.sum(d_gn * gated_rows * inv_gate, axis=0))
    scaled = d_gn * norm_scale[None, :]
    d_gated = inv_gate * scaled - gated_rows * inv_gate ** 3 * lax.optimization_barrier(jnp.mean(scaled * gated_rows, axis=1, keepdims=True))
    d_ssd = d_gated * gate_in * sig_z
    d_z = d_gated * ssd_flat * sig_z * (1.0 + gate_in * (1.0 - sig_z))
    d_xh, d_b, d_c, d_step, d_rates, g_d_skip = pull_ssd(d_ssd.reshape(row_count, head_count, HEADDIM))
    g_a_log = d_rates * decay_rates
    d_dt_raw = d_step * jax.nn.sigmoid(dt_raw + dt_bias[None, :])
    g_dt_bias = lax.optimization_barrier(jnp.sum(d_dt_raw, axis=0))
    d_act = jnp.concatenate([d_xh.reshape(row_count, inner_total), d_b, d_c], axis=1)
    _, pull_conv = jax.vjp(conv_act, padded, conv_w, conv_b)
    d_padded, g_conv_w, g_conv_b = pull_conv(d_act)
    d_pre = d_padded[CONV - 1:]
    d_zx = jnp.concatenate([d_z, d_pre[:, :inner_total]], axis=1).astype(jnp.bfloat16)
    d_dtb = d_dt_raw.astype(jnp.bfloat16)
    d_bcb = d_pre[:, inner_total:].astype(jnp.bfloat16)
    g_w_zx = jnp.dot(normed.T, d_zx, preferred_element_type=jnp.float32).reshape(w_zx.shape)
    g_w_dt = jnp.dot(normed.T, d_dtb, preferred_element_type=jnp.float32)
    g_w_bc = jnp.dot(normed.T, d_bcb, preferred_element_type=jnp.float32)
    d_normed = jnp.dot(d_zx, flat_weight.T, preferred_element_type=jnp.float32) + jnp.dot(d_dtb, w_dt.T, preferred_element_type=jnp.float32) + jnp.dot(d_bcb, w_bc.T, preferred_element_type=jnp.float32)
    g_in_gain = lax.optimization_barrier(jnp.sum(d_normed * input_float * inv_rms, axis=0))
    weighted = d_normed * in_gain[None, :]
    d_x_in = cotangent.astype(jnp.float32) + inv_rms * weighted - input_float * inv_rms ** 3 * lax.optimization_barrier(jnp.mean(weighted * input_float, axis=1, keepdims=True))
    return (y_out, d_x_in, g_in_gain, g_w_zx, g_w_dt, g_w_bc, g_conv_w[:, :inner_total], g_conv_b[:inner_total], g_conv_w[:, inner_total:], g_conv_b[inner_total:], g_a_log, g_dt_bias, g_d_skip, g_norm_scale, g_w_out)
```

```python
import functools

import jax
import jax.numpy as jnp
from jax import lax
from jax.experimental import pallas as pl
from jax.experimental.pallas import tpu as pltpu
from jax.sharding import PartitionSpec as P

HEADDIM = 64
CONV = 4
EPSILON = 1e-05
HALO = 16
BLK = 128
LANES = 128
F32 = jnp.float32
BF16 = jnp.bfloat16

PARAMS = pltpu.CompilerParams(vmem_limit_bytes=48 * 1024 * 1024)


def bits_of(axis):
    length = lax.axis_size(axis)
    return [1 << k for k in range(length.bit_length() - 1)]


def xor_permute(array, axis, bit):
    length = lax.axis_size(axis)
    return lax.ppermute(array, axis, [(i, i ^ bit) for i in range(length)])


def has_bit(axis, bit):
    return (lax.axis_index(axis) & bit) != 0


def gather_pieces(own, axis):
    pieces = {0: own}
    for bit in reversed(bits_of(axis)):
        for j in sorted(pieces):
            pieces[j | bit] = xor_permute(pieces[j], axis, bit)
    return [pieces[j] for j in sorted(pieces)]


def gather_edges(edge):
    head_size, seq_size = lax.axis_size("head"), lax.axis_size("seq")
    pieces = {}
    for j in range(0, head_size, 2):
        pairs = [
            (s * head_size + h, (s + 1) * head_size + (h ^ j))
            for s in range(seq_size - 1)
            for h in range(head_size)
        ]
        pieces[j] = lax.ppermute(edge, ("seq", "head"), pairs)
    for j in range(0, head_size, 2):
        pieces[j | 1] = xor_permute(pieces[j], "head", 1)
    return [pieces[j] for j in sorted(pieces)]


def scatter_sum(blocks, axis):
    held = dict(enumerate(blocks))
    for bit in bits_of(axis):
        upper = has_bit(axis, bit)
        low = [i for i in sorted(held) if not i & bit]
        send = [jnp.where(upper, held[i], held[i | bit]) for i in low]
        keep = [jnp.where(upper, held[i | bit], held[i]) for i in low]
        moved = [xor_permute(part, axis, bit) for part in send]
        held = {i: a + b for i, a, b in zip(low, keep, moved)}
    return held[0]


def pack(array, power):
    body = (array * jnp.exp2(-power)).astype(jnp.float16)
    note = jnp.broadcast_to(power.astype(jnp.float16), (HALO, array.shape[1]))
    return jnp.concatenate([body, note], axis=0)


def unpack(message):
    power = message[-1, 0].astype(F32)
    return message[:-HALO].astype(F32) * jnp.exp2(power), power


def all_sum_rows(array, axis, order):
    size = lax.axis_size(axis)
    part = array.shape[0] // size
    top = jnp.maximum(jnp.max(jnp.abs(array)), 1e-30)
    power = jnp.ceil(jnp.log2(top)) - 13.0
    for bit in order:
        upper = has_bit(axis, bit).astype(jnp.int32)
        half = array.shape[0] // 2
        send = lax.dynamic_slice_in_dim(array, (1 - upper) * half, half, 0)
        keep = lax.dynamic_slice_in_dim(array, upper * half, half, 0)
        moved, other = unpack(xor_permute(pack(send, power), axis, bit))
        array = keep + moved
        power = jnp.maximum(power, other) + 1.0
    held = pack(array, power)
    for bit in reversed(order):
        upper = has_bit(axis, bit)
        moved = xor_permute(held, axis, bit)
        held = jnp.concatenate(
            [jnp.where(upper, moved, held), jnp.where(upper, held, moved)], axis=0
        )
    held = held.reshape(size, part + HALO, held.shape[1])
    scale = jnp.exp2(held[:, part : part + 1, :1].astype(F32))
    return (held[:, :part].astype(F32) * scale).reshape(size * part, held.shape[2])


def all_sum_small(array, axis):
    for bit in bits_of(axis):
        array = array + xor_permute(array, axis, bit)
    return array


def state_prefix(message, axis, reverse):
    inner = message.shape[0] - 8
    before = jnp.zeros((inner, message.shape[1]), F32)
    before_log = jnp.zeros((8, message.shape[1]), F32)
    bits = bits_of(axis)
    for bit in bits:
        moved = xor_permute(message, axis, bit)
        upper = has_bit(axis, bit)
        late = jnp.logical_not(upper) if reverse else upper
        flag = late.astype(jnp.int32).reshape(1)
        before, before_log, message = call(
            prefix_kernel,
            [(before.shape, F32), (before_log.shape, F32), (message.shape, F32)],
            [flag, moved, message, before, before_log],
        )
    return before


def dg(a, b, ca, cb):
    return lax.dot_general(a, b, (((ca,), (cb,)), ((), ())), preferred_element_type=F32)


def split2(value):
    high = value.astype(BF16)
    return high, (value - high.astype(F32)).astype(BF16)


def split3(value):
    high = value.astype(BF16)
    rest = value - high.astype(F32)
    mid = rest.astype(BF16)
    return high, mid, (rest - mid.astype(F32)).astype(BF16)


def dot_left2(a, b, ca, cb):
    high, low = split2(a)
    return dg(high, b, ca, cb) + dg(low, b, ca, cb)


def dot_right2(a, b, ca, cb):
    high, low = split2(b)
    return dg(a, high, ca, cb) + dg(a, low, ca, cb)


def dot_both(a, b, ca, cb):
    a_high, a_low = split2(a)
    b_high, b_low = split2(b)
    return dg(a_high, b_high, ca, cb) + (dg(a_low, b_high, ca, cb) + dg(a_high, b_low, ca, cb))


def lane_pick(shape):
    return lax.broadcasted_iota(jnp.int32, shape, 1) < HEADDIM


def pair_lanes(columns, pair):
    rows = columns.shape[0]
    return jnp.where(
        lane_pick((rows, LANES)),
        jnp.broadcast_to(columns[:, 2 * pair : 2 * pair + 1], (rows, LANES)),
        jnp.broadcast_to(columns[:, 2 * pair + 1 : 2 * pair + 2], (rows, LANES)),
    )


def call(kernel, outs, args, scratch=(), cost=None):
    specs = []
    for arg in args:
        small = arg.dtype == jnp.int32
        specs.append(pl.BlockSpec(memory_space=pltpu.SMEM if small else pltpu.VMEM))
    return pl.pallas_call(
        kernel,
        out_shape=tuple(jax.ShapeDtypeStruct(shape, dtype) for shape, dtype in outs),
        in_specs=specs,
        out_specs=tuple(pl.BlockSpec(memory_space=pltpu.VMEM) for _ in outs),
        scratch_shapes=list(scratch),
        compiler_params=PARAMS,
        cost_estimate=cost,
    )(*args)


def prefix_kernel(late_ref, moved_ref, own_ref, before_ref, log_ref, out_ref, olog_ref, next_ref):
    inner, state = before_ref.shape
    late = late_ref[0] != 0
    own_log = own_ref[inner : inner + 1, :]
    other_log = moved_ref[inner : inner + 1, :]
    before_log = log_ref[0:1, :]
    olog_ref[...] = jnp.broadcast_to(
        jnp.where(late, jnp.maximum(before_log + other_log, -1000.0), before_log), log_ref.shape
    )
    next_ref[inner:, :] = jnp.broadcast_to(
        jnp.maximum(own_log + other_log, -1000.0), (next_ref.shape[0] - inner, state)
    )
    add_row = jnp.where(late, jnp.exp(before_log), 0.0)
    other_row = jnp.where(late, jnp.exp(own_log), 1.0)
    own_row = jnp.where(late, 1.0, jnp.exp(other_log))
    for r in range(0, inner, BLK):
        member = (
            lax.broadcasted_iota(jnp.int32, (BLK, state), 0) // HEADDIM + r // HEADDIM
            == lax.broadcasted_iota(jnp.int32, (BLK, state), 1)
        )
        pick = lambda row: jnp.sum(jnp.where(member, row, 0.0), axis=1, keepdims=True)
        other = moved_ref[r : r + BLK, :]
        out_ref[r : r + BLK, :] = before_ref[r : r + BLK, :] + pick(add_row) * other
        next_ref[r : r + BLK, :] = (
            pick(own_row) * own_ref[r : r + BLK, :] + pick(other_row) * other
        )


def project_kernel(count, *refs):
    me_ref = refs[0]
    main = refs[1 : 1 + count]
    halo = refs[1 + count : 1 + 2 * count]
    (gain_ref, wzx_ref, w2_ref, tap_ref, bias_ref, rate_ref, dtb_ref) = refs[
        1 + 2 * count : 8 + 2 * count
    ]
    (nb_ref, inv_ref, z_ref, pre_ref, conv_ref, act_ref, a_ref, at_ref, step_ref, stept_ref,
     dtr_ref, sloc_ref) = refs[8 + 2 * count : 20 + 2 * count]
    xf, nball, pre32 = refs[20 + 2 * count :]
    rows = z_ref.shape[0]
    inner = z_ref.shape[1]
    width = main[0].shape[1]
    state = sloc_ref.shape[1]
    channels = inner + 2 * state
    me = me_ref[0]
    for j in range(count):
        at = pl.multiple_of((me ^ j) * width, LANES)
        xf[0:HALO, pl.ds(at, width)] = halo[j][...]
        xf[HALO : HALO + rows, pl.ds(at, width)] = main[j][...]
    gain = gain_ref[...]
    starts = [0] + list(range(HALO, HALO + rows, BLK))
    for start in starts:
        size = HALO if start == 0 else BLK
        value = xf[start : start + size, :].astype(F32)
        inv = lax.rsqrt(jnp.mean(value * value, axis=1, keepdims=True) + EPSILON)
        normed = (value * inv * gain).astype(BF16)
        nball[start : start + size, :] = normed
        if start:
            nb_ref[start - HALO : start - HALO + size, :] = normed
            inv_ref[start - HALO : start - HALO + size, :] = inv
    weights2 = w2_ref[...]
    for start in starts:
        size = HALO if start == 0 else BLK
        left = nball[start : start + size, :]
        zx = jnp.dot(left, wzx_ref[...], preferred_element_type=F32)
        rest = jnp.dot(left, weights2, preferred_element_type=F32)
        xs = zx[:, inner:].astype(BF16)
        bc = rest[:, : 2 * state].astype(BF16)
        pre_ref[start : start + size, :inner] = xs
        pre_ref[start : start + size, inner:] = bc
        pre32[start : start + size, :inner] = xs.astype(F32)
        pre32[start : start + size, inner:] = bc.astype(F32)
        if start:
            at = start - HALO
            z_ref[at : at + size, :] = zx[:, :inner].astype(BF16)
            dtr_ref[at : at + size, :] = rest[:, 2 * state :] + dtb_ref[...]
    for c in range(0, channels, LANES):
        for r in range(0, rows, BLK):
            total = jnp.broadcast_to(bias_ref[:, c : c + LANES], (BLK, LANES))
            for k in range(CONV):
                first = HALO - (CONV - 1) + k + r
                total = total + tap_ref[k : k + 1, c : c + LANES] * pre32[
                    first : first + BLK, c : c + LANES
                ]
            conv_ref[r : r + BLK, c : c + LANES] = total
            act_ref[r : r + BLK, c : c + LANES] = (total * jax.nn.sigmoid(total)).astype(BF16)
    raw = dtr_ref[...]
    step = jnp.maximum(raw, 0.0) + jnp.log1p(jnp.exp(-jnp.abs(raw)))
    step_ref[...] = step
    stept_ref[...] = step.T
    lower = (
        lax.broadcasted_iota(jnp.int32, (rows, rows), 0)
        >= lax.broadcasted_iota(jnp.int32, (rows, rows), 1)
    ).astype(F32).astype(BF16)
    high, mid, low = split3(step * rate_ref[...])
    total = dg(lower, high, 1, 0) + (dg(lower, mid, 1, 0) + dg(lower, low, 1, 0))
    a_ref[...] = total
    at_ref[...] = total.T
    weight = jnp.exp(total[rows - 1 : rows, :] - total) * step
    sloc_ref[inner:, :] = jnp.broadcast_to(
        jnp.maximum(total[rows - 1 : rows, :], -1000.0), (sloc_ref.shape[0] - inner, LANES)
    )
    b_vals = act_ref[:, inner : inner + state]
    for pair in range(inner // LANES):
        c = pair * LANES
        weighted = act_ref[:, c : c + LANES].astype(F32) * pair_lanes(weight, pair)
        sloc_ref[c : c + LANES, :] = dot_left2(weighted, b_vals, 0, 0)


def within_kernel(act_ref, a_ref, at_ref, stept_ref, skip_ref, y_ref, scores):
    rows, inner = y_ref.shape
    state = (act_ref.shape[1] - inner) // 2
    for r in range(0, rows, BLK):
        scores[r : r + BLK, : r + BLK] = dg(
            act_ref[r : r + BLK, inner + state :], act_ref[: r + BLK, inner : inner + state], 1, 1
        )
    causal = lax.broadcasted_iota(jnp.int32, (BLK, BLK), 0) >= lax.broadcasted_iota(
        jnp.int32, (BLK, BLK), 1
    )
    pick = lane_pick((BLK, LANES))
    for pair in range(inner // LANES):
        c = pair * LANES
        for r in range(0, rows, BLK):
            results = []
            for h in (2 * pair, 2 * pair + 1):
                column = a_ref[r : r + BLK, h : h + 1]
                parts = []
                for s in range(0, r + BLK, BLK):
                    spread = column - at_ref[h : h + 1, s : s + BLK]
                    if s == r:
                        spread = jnp.where(causal, spread, -1e30)
                    parts.append(
                        scores[r : r + BLK, s : s + BLK]
                        * jnp.exp(spread)
                        * stept_ref[h : h + 1, s : s + BLK]
                    )
                mixing = jnp.concatenate(parts, axis=1) if len(parts) > 1 else parts[0]
                results.append(dot_left2(mixing, act_ref[: r + BLK, c : c + LANES], 1, 0))
            x_part = act_ref[r : r + BLK, c : c + LANES].astype(F32)
            y_ref[r : r + BLK, c : c + LANES] = (
                jnp.where(pick, results[0], results[1]) + skip_ref[:, c : c + LANES] * x_part
            )


def cotangent_kernel(count, *refs):
    me_ref = refs[0]
    main = refs[1 : 1 + count]
    w_ref, full_ref, dgn_ref = refs[1 + count :]
    width = main[0].shape[1]
    me = me_ref[0]
    for j in range(count):
        at = pl.multiple_of((me ^ j) * width, LANES)
        full_ref[:, pl.ds(at, width)] = main[j][...]
    dgn_ref[...] = dg(full_ref[...], w_ref[...], 1, 1)


def gate_kernel(yl_ref, act_ref, a_ref, sin_ref, z_ref, dgn_ref, ns_ref, y_ref, sums_ref):
    rows, inner = y_ref.shape
    state = sin_ref.shape[1]
    for r in range(0, rows, BLK):
        reach = dot_right2(act_ref[r : r + BLK, inner + state :], sin_ref[...], 1, 1)
        grow = jnp.exp(a_ref[r : r + BLK, :])
        squares = jnp.zeros((BLK, LANES), F32)
        inners = jnp.zeros((BLK, LANES), F32)
        for pair in range(inner // LANES):
            c = pair * LANES
            y = yl_ref[r : r + BLK, c : c + LANES] + pair_lanes(grow, pair) * reach[:, c : c + LANES]
            y_ref[r : r + BLK, c : c + LANES] = y
            z = z_ref[r : r + BLK, c : c + LANES].astype(F32)
            gated = y * z * jax.nn.sigmoid(z)
            squares = squares + gated * gated
            inners = inners + dgn_ref[r : r + BLK, c : c + LANES] * ns_ref[:, c : c + LANES] * gated
        lane = lax.broadcasted_iota(jnp.int32, (BLK, LANES), 1)
        both = jnp.where(
            lane == 0,
            jnp.sum(squares, axis=1, keepdims=True),
            jnp.where(lane == 1, jnp.sum(inners, axis=1, keepdims=True), 0.0),
        )
        sums_ref[:, r : r + BLK] = both.T[:8, :]


def gate_back_kernel(
    inner_total, y_ref, z_ref, dgn_ref, ns_ref, sums_ref, act_ref, a_ref,
    gn_ref, dy_ref, dz_ref, rows_ref, reach_ref, grown,
):
    rows, inner = y_ref.shape
    state = reach_ref.shape[1]
    rows_ref[...] = jnp.zeros_like(rows_ref)
    for r in range(0, rows, BLK):
        padded = jnp.concatenate(
            [sums_ref[:, r : r + BLK], jnp.zeros((LANES - 8, BLK), F32)], axis=0
        ).T
        inv = lax.rsqrt(padded[:, 0:1] / inner_total + EPSILON)
        pull = inv * inv * inv * (padded[:, 1:2] / inner_total)
        grow = jnp.exp(a_ref[r : r + BLK, :])
        for pair in range(inner // LANES):
            c = pair * LANES
            y = y_ref[r : r + BLK, c : c + LANES]
            z = z_ref[r : r + BLK, c : c + LANES].astype(F32)
            dgn = dgn_ref[r : r + BLK, c : c + LANES]
            scale = ns_ref[:, c : c + LANES]
            sig = jax.nn.sigmoid(z)
            gated = y * z * sig
            base = gated * inv
            gn_ref[r : r + BLK, c : c + LANES] = (base * scale).astype(BF16)
            d_gated = inv * (dgn * scale) - gated * pull
            d_y = d_gated * z * sig
            dy_ref[r : r + BLK, c : c + LANES] = d_y
            grown[r : r + BLK, c : c + LANES] = d_y * pair_lanes(grow, pair)
            dz_ref[r : r + BLK, c : c + LANES] = (
                d_gated * y * sig * (1.0 + z * (1.0 - sig))
            ).astype(BF16)
            x = act_ref[r : r + BLK, c : c + LANES].astype(F32)
            rows_ref[0:1, c : c + LANES] += jnp.sum(dgn * base, axis=0, keepdims=True)
            rows_ref[1:2, c : c + LANES] += jnp.sum(d_y * x, axis=0, keepdims=True)
    c_vals = act_ref[:, inner + state :]
    reach_ref[inner:, :] = jnp.broadcast_to(
        jnp.maximum(a_ref[rows - 1 : rows, :], -1000.0), (reach_ref.shape[0] - inner, LANES)
    )
    for c in range(0, inner, LANES):
        reach_ref[c : c + LANES, :] = dot_left2(grown[:, c : c + LANES], c_vals, 0, 0)


def back_kernel(
    act_ref, a_ref, at_ref, step_ref, dy_ref, sin_ref,
    dx_ref, db_ref, dc_ref, dsd_ref, dat_ref, dea_ref, scores, dscores, dyh, dyl,
):
    rows, inner = dx_ref.shape
    state = sin_ref.shape[1]
    dsd_ref[...] = jnp.zeros_like(dsd_ref)
    dat_ref[...] = jnp.zeros_like(dat_ref)
    dea_ref[...] = jnp.zeros_like(dea_ref)
    for r in range(0, rows, BLK):
        high, low = split2(dy_ref[r : r + BLK, :])
        dyh[r : r + BLK, :] = high
        dyl[r : r + BLK, :] = low
        scores[r : r + BLK, r:] = dg(
            act_ref[r : r + BLK, inner : inner + state], act_ref[r:, inner + state :], 1, 1
        )
        dscores[r : r + BLK, r:] = jnp.zeros((BLK, rows - r), F32)
    causal = lax.broadcasted_iota(jnp.int32, (BLK, BLK), 1) >= lax.broadcasted_iota(
        jnp.int32, (BLK, BLK), 0
    )
    pick = lane_pick((BLK, LANES))
    for pair in range(inner // LANES):
        c = pair * LANES
        for s in range(0, rows, BLK):
            results = []
            x_pair = act_ref[s : s + BLK, c : c + LANES]
            for which in range(2):
                h = 2 * pair + which
                a_col = a_ref[s : s + BLK, h : h + 1]
                s_col = step_ref[s : s + BLK, h : h + 1]
                mine = pick if which == 0 else jnp.logical_not(pick)
                x_only = jnp.where(mine, x_pair.astype(F32), 0.0).astype(BF16)
                d_mix = dg(x_only, dyh[s:, c : c + LANES], 1, 1) + dg(
                    x_only, dyl[s:, c : c + LANES], 1, 1
                )
                parts = []
                row_sum = jnp.zeros((BLK, BLK), F32)
                for t in range(s, rows, BLK):
                    spread = at_ref[h : h + 1, t : t + BLK] - a_col
                    if s == t:
                        spread = jnp.where(causal, spread, -1e30)
                    decay = jnp.exp(spread)
                    kernel = scores[s : s + BLK, t : t + BLK] * decay
                    d_part = d_mix[:, t - s : t - s + BLK]
                    edge = d_part * kernel
                    row_sum = row_sum + edge
                    dat_ref[h : h + 1, t : t + BLK] += jnp.sum(
                        edge * s_col, axis=0, keepdims=True
                    )
                    dscores[s : s + BLK, t : t + BLK] += d_part * (decay * s_col)
                    parts.append(kernel * s_col)
                dsd_ref[s : s + BLK, h : h + 1] = jnp.sum(row_sum, axis=1, keepdims=True)
                mixing = jnp.concatenate(parts, axis=1) if len(parts) > 1 else parts[0]
                high, low = split2(mixing)
                right = dyh[s:, c : c + LANES]
                results.append(
                    dg(high, right, 1, 0)
                    + (dg(low, right, 1, 0) + dg(high, dyl[s:, c : c + LANES], 1, 0))
                )
            dx_ref[s : s + BLK, c : c + LANES] = jnp.where(pick, results[0], results[1])
    for r in range(0, rows, BLK):
        high, low = split2(dscores[r : r + BLK, r:])
        c_after = act_ref[r:, inner + state :]
        db_ref[r : r + BLK, :] = dg(high, c_after, 1, 0) + dg(low, c_after, 1, 0)
    for t in range(0, rows, BLK):
        high, low = split2(dscores[: t + BLK, t : t + BLK])
        b_before = act_ref[: t + BLK, inner : inner + state]
        grow = jnp.exp(a_ref[t : t + BLK, :])
        reach = dot_right2(act_ref[t : t + BLK, inner + state :], sin_ref[...], 1, 1)
        lane = lax.broadcasted_iota(jnp.int32, (BLK, LANES), 1)
        grown, columns = [], jnp.zeros((BLK, LANES), F32)
        for pair in range(inner // LANES):
            c = pair * LANES
            d_y = dy_ref[t : t + BLK, c : c + LANES]
            grown.append(d_y * pair_lanes(grow, pair))
            product = d_y * reach[:, c : c + LANES]
            first = jnp.sum(jnp.where(pick, product, 0.0), axis=1, keepdims=True)
            second = jnp.sum(jnp.where(pick, 0.0, product), axis=1, keepdims=True)
            columns = jnp.where(
                lane == 2 * pair, first, jnp.where(lane == 2 * pair + 1, second, columns)
            )
        dea_ref[t : t + BLK, :] = columns * grow
        dc_ref[t : t + BLK, :] = (
            dg(high, b_before, 0, 0)
            + dg(low, b_before, 0, 0)
            + dot_both(jnp.concatenate(grown, axis=1), sin_ref[...], 1, 0)
        )


def finish_kernel(
    act_ref, a_ref, step_ref, dy_ref, sin_ref, r_ref, dx_ref, db_ref, dsd_ref, dat_ref, dea_ref,
    conv_ref, pre_ref, dtr_ref, rate_ref, skip_ref,
    dbo_ref, dconv_ref, taps_ref, ddt_ref, heads_ref, pre32,
):
    rows, inner = dx_ref.shape
    state = sin_ref.shape[1]
    a = a_ref[...]
    step = step_ref[...]
    last = a[rows - 1 : rows, :]
    decay = jnp.exp(last - a)
    weight = decay * step
    pre32[...] = pre_ref[:, :inner].astype(F32)
    taps_ref[...] = jnp.zeros_like(taps_ref)
    lane = lax.broadcasted_iota(jnp.int32, (BLK, LANES), 1)
    pick = lane_pick((BLK, LANES))
    d_weight = []
    for r in range(0, rows, BLK):
        back = dot_right2(act_ref[r : r + BLK, inner : inner + state], r_ref[...], 1, 1)
        columns = jnp.zeros((BLK, LANES), F32)
        weighted = []
        for pair in range(inner // LANES):
            c = pair * LANES
            x = act_ref[r : r + BLK, c : c + LANES].astype(F32)
            over = pair_lanes(weight[r : r + BLK, :], pair)
            v = back[:, c : c + LANES]
            weighted.append(over * x)
            product = x * v
            first = jnp.sum(jnp.where(pick, product, 0.0), axis=1, keepdims=True)
            second = jnp.sum(jnp.where(pick, 0.0, product), axis=1, keepdims=True)
            columns = jnp.where(
                lane == 2 * pair, first, jnp.where(lane == 2 * pair + 1, second, columns)
            )
            d_x = (
                dx_ref[r : r + BLK, c : c + LANES]
                + skip_ref[:, c : c + LANES] * dy_ref[r : r + BLK, c : c + LANES]
                + over * v
            )
            value = conv_ref[r : r + BLK, c : c + LANES]
            sig = jax.nn.sigmoid(value)
            d_conv = d_x * (sig * (1.0 + value * (1.0 - sig)))
            dconv_ref[r : r + BLK, c : c + LANES] = d_conv
            for k in range(CONV):
                first_row = HALO - (CONV - 1) + k + r
                taps_ref[k : k + 1, c : c + LANES] += jnp.sum(
                    d_conv * pre32[first_row : first_row + BLK, c : c + LANES],
                    axis=0,
                    keepdims=True,
                )
            taps_ref[CONV : CONV + 1, c : c + LANES] += jnp.sum(d_conv, axis=0, keepdims=True)
        d_weight.append(columns)
        dbo_ref[r : r + BLK, :] = db_ref[r : r + BLK, :] + dot_both(
            jnp.concatenate(weighted, axis=1), r_ref[...], 1, 0
        )
    d_weight = jnp.concatenate(d_weight, axis=0)
    product = r_ref[...] * sin_ref[...]
    high, mid, low = split3(product)
    ones = jnp.ones((8, state), F32).astype(BF16)
    sums = dg(ones, high, 1, 1) + (dg(ones, mid, 1, 1) + dg(ones, low, 1, 1))
    member = (
        lax.broadcasted_iota(jnp.int32, (inner, LANES), 0) // HEADDIM
        == lax.broadcasted_iota(jnp.int32, (inner, LANES), 1)
    ).astype(F32).astype(BF16)
    high, mid, low = split3(sums)
    dots = dg(high, member, 1, 0) + (dg(mid, member, 1, 0) + dg(low, member, 1, 0))
    passed = weight * d_weight
    d_last = jnp.sum(passed, axis=0, keepdims=True) + jnp.exp(last) * dots[0:1, :]
    dat = jnp.concatenate(
        [dat_ref[...], jnp.zeros((LANES - dat_ref.shape[0], rows), F32)], axis=0
    ).T
    d_a = dat - step * dsd_ref[...] + dea_ref[...] - passed
    is_last = lax.broadcasted_iota(jnp.int32, (rows, LANES), 0) == rows - 1
    d_a = d_a + jnp.where(is_last, d_last, 0.0)
    upper = (
        lax.broadcasted_iota(jnp.int32, (rows, rows), 1)
        >= lax.broadcasted_iota(jnp.int32, (rows, rows), 0)
    ).astype(F32).astype(BF16)
    high, mid, low = split3(d_a)
    d_log = dg(upper, high, 1, 0) + (dg(upper, mid, 1, 0) + dg(upper, low, 1, 0))
    rate = rate_ref[...]
    d_step = dsd_ref[...] + decay * d_weight + rate * d_log
    d_raw = d_step * jax.nn.sigmoid(dtr_ref[...])
    ddt_ref[...] = d_raw.astype(BF16)
    heads_ref[...] = jnp.zeros_like(heads_ref)
    heads_ref[0:1, :] = jnp.sum(step * d_log, axis=0, keepdims=True) * rate
    heads_ref[1:2, :] = jnp.sum(d_raw, axis=0, keepdims=True)


def pad_lanes(array):
    return jnp.pad(array, ((0, 0), (0, LANES - array.shape[1])))


def narrow(array, axis, dim):
    for bit in bits_of(axis):
        low, high = jnp.split(array, 2, axis=dim)
        array = jnp.where(has_bit(axis, bit), high, low)
    return array


def widen(array, axis, dim):
    for bit in reversed(bits_of(axis)):
        moved = xor_permute(array, axis, bit)
        upper = has_bit(axis, bit)
        array = jnp.concatenate(
            [jnp.where(upper, moved, array), jnp.where(upper, array, moved)], axis=dim
        )
    return array


def conv_sum(padded, weights, reverse):
    rows = padded.shape[0] - (CONV - 1)
    total = 0.0
    for k in range(CONV):
        first = CONV - 1 - k if reverse else k
        total = total + weights[k][None, :] * padded[first : first + rows]
    return total


def local(
    x_in, in_gain, w_zx, w_dt, w_bc, conv_x, conv_x_bias, conv_bc, conv_bc_bias,
    a_log, dt_bias, d_skip, norm_scale, w_out, cotangent,
):
    rows, slice_width = x_in.shape
    width, _, inner = w_zx.shape
    head_count = w_dt.shape[1]
    state = w_bc.shape[1] // 2
    channels = inner + 2 * state
    head_size, seq_size = lax.axis_size("head"), lax.axis_size("seq")
    inner_total = inner * head_size
    me = lax.axis_index("head")
    me_arr = me.astype(jnp.int32).reshape(1)

    x_pieces = gather_pieces(x_in, "head")
    halos = gather_edges(x_in[rows - HALO :])
    c_pieces = gather_pieces(cotangent, "head")

    flat = w_zx.reshape(width, 2 * inner)
    w_small = jnp.concatenate([w_bc, pad_lanes(w_dt)], axis=1)
    conv_w = jnp.concatenate([conv_x, conv_bc], axis=1)
    conv_b = jnp.concatenate([conv_x_bias, conv_bc_bias])[None, :]
    rates = -jnp.exp(a_log)
    rate_row = pad_lanes(rates[None, :])
    dtb_row = pad_lanes(dt_bias[None, :])
    skip_row = jnp.repeat(d_skip, HEADDIM)[None, :]
    scale_row = norm_scale[None, :]

    nb, inv_rms, z, pre, conv, act, a, at, step, stept, dtr, sloc = call(
        functools.partial(project_kernel, head_size),
        [
            ((rows, width), BF16),
            ((rows, 1), F32),
            ((rows, inner), BF16),
            ((rows + HALO, channels), BF16),
            ((rows, channels), F32),
            ((rows, channels), BF16),
            ((rows, LANES), F32),
            ((LANES, rows), F32),
            ((rows, LANES), F32),
            ((LANES, rows), F32),
            ((rows, LANES), F32),
            ((inner + 8, state), F32),
        ],
        [me_arr, *x_pieces, *halos, in_gain[None, :], flat, w_small, conv_w, conv_b, rate_row, dtb_row],
        [
            pltpu.VMEM((rows + HALO, width), BF16),
            pltpu.VMEM((rows + HALO, width), BF16),
            pltpu.VMEM((rows + HALO, channels), F32),
        ],
    )
    state_in = state_prefix(sloc, "seq", False)
    (y_local,) = call(
        within_kernel,
        [((rows, inner), F32)],
        [act, a, at, stept, skip_row],
        [pltpu.VMEM((rows, rows), F32)],
    )
    cot_full, d_gn = call(
        functools.partial(cotangent_kernel, head_size),
        [((rows, width), BF16), ((rows, inner), F32)],
        [me_arr, *c_pieces, w_out],
    )
    y, sums = call(
        gate_kernel,
        [((rows, inner), F32), ((8, rows), F32)],
        [y_local, act, a, state_in, z, d_gn, scale_row],
    )
    sums = sums + sum(
        lax.ppermute(sums, "head", [(i, i ^ j) for i in range(head_size)])
        for j in range(1, head_size)
    )
    gate_normed, d_y, d_z, gate_rows, reach = call(
        functools.partial(gate_back_kernel, inner_total),
        [
            ((rows, inner), BF16),
            ((rows, inner), F32),
            ((rows, inner), BF16),
            ((8, inner), F32),
            ((inner + 8, state), F32),
        ],
        [y, z, d_gn, scale_row, sums, act, a],
        [pltpu.VMEM((rows, inner), F32)],
    )
    state_grad = state_prefix(reach, "seq", True)

    partial_out = jnp.dot(gate_normed, w_out, preferred_element_type=F32)
    out_slice = scatter_sum(jnp.split(partial_out, head_size, axis=1), "head")
    y_out = (x_in.astype(F32) + out_slice).astype(BF16)

    over_rows = (((0,), (0,)), ((), ()))
    g_w_out = lax.dot_general(gate_normed, cot_full, over_rows, preferred_element_type=F32)
    g_w_z = lax.dot_general(nb, d_z, over_rows, preferred_element_type=F32)
    seq_bits = bits_of("seq")
    turned = seq_bits[1:] + seq_bits[:1]
    s_out = all_sum_rows(g_w_out, "seq", seq_bits)
    s_z = all_sum_rows(g_w_z, "seq", turned)

    dx, db, dc, dsd, dat, dea = call(
        back_kernel,
        [
            ((rows, inner), F32),
            ((rows, state), F32),
            ((rows, state), F32),
            ((rows, LANES), F32),
            ((8, rows), F32),
            ((rows, LANES), F32),
        ],
        [act, a, at, step, d_y, state_in],
        [
            pltpu.VMEM((rows, rows), F32),
            pltpu.VMEM((rows, rows), F32),
            pltpu.VMEM((rows, inner), BF16),
            pltpu.VMEM((rows, inner), BF16),
        ],
    )
    db, d_conv_x, tap_rows, d_dtb, head_rows = call(
        finish_kernel,
        [
            ((rows, state), F32),
            ((rows, inner), F32),
            ((8, inner), F32),
            ((rows, LANES), BF16),
            ((8, LANES), F32),
        ],
        [act, a, step, d_y, state_in, state_grad, dx, db, dsd, dat, dea,
         conv, pre, dtr, rate_row, skip_row],
        [pltpu.VMEM((rows + HALO, inner), F32)],
    )

    d_bc = jnp.concatenate([db, dc], axis=1)
    for bit in bits_of("head"):
        low, high = jnp.split(d_bc, 2, axis=1)
        upper = has_bit("head", bit)
        send = jnp.where(upper, low, high)
        d_bc = jnp.where(upper, high, low) + xor_permute(send, "head", bit)
    conv_part = narrow(conv[:, inner:], "head", 1)
    sig = jax.nn.sigmoid(conv_part)
    d_conv_bc = d_bc * (sig * (1.0 + conv_part * (1.0 - sig)))
    pre_part = narrow(pre[HALO - (CONV - 1) :, inner:], "head", 1).astype(F32)
    g_conv_bc = jnp.stack(
        [jnp.sum(d_conv_bc * pre_part[k : k + rows], axis=0) for k in range(CONV)]
        + [jnp.sum(d_conv_bc, axis=0)]
    )
    part = d_bc.shape[1]
    back_pairs = [(i, i - 1) for i in range(1, seq_size)]
    edge_grad = lax.ppermute(
        jnp.concatenate([d_conv_x[:8], d_conv_bc[:8]], axis=1), "seq", back_pairs
    )[: CONV - 1]
    d_pre_x = conv_sum(jnp.concatenate([d_conv_x, edge_grad[:, :inner]], axis=0), conv_x, True)
    d_x_b = d_pre_x.astype(BF16)
    tap_part = narrow(conv_bc, "head", 1)
    d_pre_bc = conv_sum(jnp.concatenate([d_conv_bc, edge_grad[:, inner:]], axis=0), tap_part, True)
    d_bcb = d_pre_bc.astype(BF16)

    w_bc_part = narrow(w_bc, "head", 1)
    right = jnp.concatenate([d_z, d_x_b], axis=1)
    d_partial = jnp.dot(right, flat.T, preferred_element_type=F32)
    tail = jnp.concatenate([d_dtb[:, :head_count], d_bcb], axis=1)
    tail_w = jnp.concatenate([w_dt, w_bc_part], axis=1)
    d_partial = d_partial + jnp.dot(tail, tail_w.T, preferred_element_type=F32)
    g_w_x = lax.dot_general(nb, d_x_b, over_rows, preferred_element_type=F32)
    g_tail = lax.dot_general(tail, nb, over_rows, preferred_element_type=F32)

    x_blocks = [None] * head_size
    stacked = jnp.stack(x_pieces)
    for bit in bits_of("head"):
        grouped = stacked.reshape(head_size // (2 * bit), 2, bit, rows, slice_width)
        stacked = jnp.where(has_bit("head", bit), grouped[:, ::-1], grouped).reshape(stacked.shape)
    x_blocks = [stacked[i].astype(F32) for i in range(head_size)]
    d_blocks = jnp.split(d_partial, head_size, axis=1)
    gain_blocks = jnp.split(in_gain, head_size)
    row_total = sum(
        jnp.sum(d * g[None, :] * x, axis=1) for d, g, x in zip(d_blocks, gain_blocks, x_blocks)
    )
    row_total = lax.psum(row_total, "head")[:, None]
    d_normed = scatter_sum(d_blocks, "head")
    gain_own = lax.dynamic_slice_in_dim(in_gain, me * slice_width, slice_width, 0)
    x_own = x_in.astype(F32)
    d_x_in = cotangent.astype(F32) + (
        inv_rms * (d_normed * gain_own[None, :])
        - x_own * (inv_rms * inv_rms * inv_rms) * (row_total / width)
    )
    g_gain = jnp.sum(d_normed * x_own * inv_rms, axis=0)

    g_bc = g_tail[head_count:]
    count = width // inner
    half = width // 2
    bc_rows = jnp.concatenate(jnp.split(g_bc, count, axis=1), axis=0)
    s_low = all_sum_rows(g_w_x[:half], "seq", seq_bits)
    s_high = all_sum_rows(jnp.concatenate([g_w_x[half:], bc_rows], axis=0), "seq", turned)
    s_x = jnp.concatenate([s_low, s_high[: width - half]], axis=0)
    g_bc = jnp.concatenate(jnp.split(s_high[width - half :], count, axis=0), axis=1)

    def lanes(array, target):
        return jnp.pad(array, ((0, -array.shape[0] % 8), (0, target - array.shape[1])))

    dt_rows = jnp.concatenate(jnp.split(g_tail[:head_count], count, axis=1), axis=0)
    small = jnp.concatenate(
        [
            tap_rows,
            gate_rows,
            lanes(head_rows, inner),
            lanes(g_conv_bc, inner),
            lanes(g_gain[None, :], inner),
            dt_rows,
        ],
        axis=0,
    )
    small = all_sum_small(small, "seq")
    tap_rows, gate_rows, head_rows, g_conv_bc = small[:8], small[8:16], small[16:24], small[24:32]
    g_gain = small[32, :slice_width]
    g_w_dt = jnp.concatenate(jnp.split(small[40:], count, axis=0), axis=1).T
    g_cbc = widen(g_conv_bc[:, :part], "head", 1)
    g_w_bc = widen(g_bc, "head", 0).T
    g_w_zx = jnp.stack([s_z, s_x], axis=1)
    return (
        y_out,
        d_x_in,
        g_gain,
        g_w_zx,
        g_w_dt,
        g_w_bc,
        tap_rows[:CONV],
        tap_rows[CONV],
        g_cbc[:CONV],
        g_cbc[CONV],
        head_rows[0, :head_count],
        head_rows[1, :head_count],
        jnp.sum(gate_rows[1].reshape(head_count, HEADDIM), axis=1),
        gate_rows[0],
        s_out,
    )


def solution(mesh):
    in_specs = (
        P("seq", "head"),
        P(),
        P(None, None, "head"),
        P(None, "head"),
        P(),
        P(None, "head"),
        P("head"),
        P(),
        P(),
        P("head"),
        P("head"),
        P("head"),
        P("head"),
        P("head", None),
        P("seq", "head"),
    )
    out_specs = (
        P("seq", "head"),
        P("seq", "head"),
        P("head"),
        P(None, None, "head"),
        P(None, "head"),
        P(),
        P(None, "head"),
        P("head"),
        P(),
        P(),
        P("head"),
        P("head"),
        P("head"),
        P("head"),
        P("head", None),
    )
    return jax.shard_map(local, mesh=mesh, in_specs=in_specs, out_specs=out_specs, check_vma=False)
```
